512 devices in a mesh: row: 32 (over z_lo, y, core), col: 16 (over x, z_hi).
Axes of the slice: x: 4, y: 4, z: 16 (z_hi: 4, z_lo: 4; z = z_hi * 4 + z_lo), core: 2. Of those that a mesh axis runs over, the one named last changes fastest.
Arguments:
- features: bfloat16 [65536, 256], P(('row', 'col')), may hold values from -6 to 6
- tile_values: bfloat16 [32, 16, 32, 128, 128], P('row', 'col'), may hold values from -0.109375 to 0.109375
- tile_rows: int32 [32, 16, 32], P('row', 'col'), may hold values from 0 to 15, as said below
- tile_cols: int32 [32, 16, 32], P('row', 'col'), may hold values from 0 to 31
- tile_count: int32 [32, 16], P('row', 'col'), may hold values from 1 to 32, as said below
- weight: bfloat16 [256, 256], replicated, may hold values from -0.375 to 0.375
- out_grad: bfloat16 [65536, 256], P(('row', 'col')), may hold values from -6 to 6
Outputs:
- activated: bfloat16 [65536, 256], P(('row', 'col'))
- feature_grad: bfloat16 [65536, 256], P(('row', 'col'))
- weight_grad: float32 [256, 256], replicated
The draws below stay inside these ranges and needn't reach their ends.
Inputs may be any that keep to these rules, and one draw needn't show every extreme that they name: Within one grid cell the pairs (tile_rows, tile_cols) of all 32 slots are distinct. `tile_count`: some grid cell has all 32 slots live.
All inputs are finite; a program needn't handle non-finite values.
Results may differ from the reference program's by a relative error of at most 0.023.
Values may be sent and summed in bfloat16 or wider, within the bound.
No kernel may reach another device: no remote copies, remote signals or barrier semaphores. Data moves between devices by JAX's collectives and lax.ppermute only.
A program may use at most 64 MiB of HBM per device.

```python
import jax
import jax.numpy as jnp
from jax import lax

F = 256
TILE = 128
SB = 128
NODES = 65536
ROW_TILES = 16
COL_TILES = 32
TILES_MAX = 32
N_ROW = 32
N_COL = 16


def tile_layout(key):
    base = jax.random.fold_in(key, 7)
    cell_keys = jax.random.split(base, N_ROW * N_COL)
    orders = jax.vmap(lambda cell_key: jax.random.permutation(cell_key, ROW_TILES * COL_TILES))(cell_keys)
    return orders[:, :TILES_MAX].astype(jnp.int32).reshape(N_ROW, N_COL, TILES_MAX)


def draw_tile_rows(key, part):
    return tile_layout(key) // COL_TILES


def draw_tile_cols(key, part):
    return tile_layout(key) % COL_TILES


def draw_tile_count(key, part):
    lowest = max(1, TILES_MAX // 2)
    counts = jax.random.randint(jax.random.fold_in(key, 11), (N_ROW * N_COL,), lowest, TILES_MAX + 1, dtype=jnp.int32)
    busiest = jax.random.randint(jax.random.fold_in(key, 12), (), 0, N_ROW * N_COL, dtype=jnp.int32)
    counts = counts.at[busiest].set(TILES_MAX)
    return counts.reshape(N_ROW, N_COL)


def levels(key, shape, shards, least, top_value):
    def one(dim, shards_of):
        steps = jax.random.uniform(jax.random.fold_in(jax.random.fold_in(key, 6), dim), (shards_of,), jnp.float32, least / len(shards), top_value / len(shards))
        return jnp.repeat(jnp.exp(steps), shape[dim] // shards_of).reshape((-1,) + (1,) * (len(shape) - dim - 1))

    level = one(*shards[0])
    for cut in shards[1:]:
        level = level * one(*cut)
    return level


def centred(key, dims, width, limit, cuts=(), held_as=jnp.bfloat16):
    entries = width * jax.random.normal(key, dims, jnp.float32)
    if cuts:
        entries = entries * levels(key, dims, cuts, -0.22, 0.18)
    return jnp.clip(entries, -limit, limit).astype(held_as)


def setup_inputs(seed: int = 0) -> dict:
    splits = jax.random.split(jax.random.key(seed), 8)
    features = centred(splits[0], (NODES, F), 1.0, 6.0, ((0, 512),))
    tile_values = centred(splits[1], (N_ROW, N_COL, TILES_MAX, TILE, TILE), (max(TILE, 3 * TILES_MAX * TILE * TILE // (4 * SB))) ** -0.5, 0.109375, ((0, 32), (1, 16)))
    tile_rows = draw_tile_rows(jax.random.fold_in(splits[7], 71), 0)
    tile_cols = draw_tile_cols(jax.random.fold_in(splits[7], 71), 0)
    tile_count = draw_tile_count(jax.random.fold_in(splits[7], 71), 0)
    weight = centred(splits[5], (F, F), F ** -0.5, 0.375)
    out_grad = centred(splits[6], (NODES, F), 1.0, 6.0, ((0, 512),))
    return dict(features=features, tile_values=tile_values, tile_rows=tile_rows, tile_cols=tile_cols, tile_count=tile_count, weight=weight, out_grad=out_grad)


def gelu_value(preact):
    return jax.nn.gelu(preact, approximate=True)

def gelu_backward(preact, upstream):
    _, pullback = jax.vjp(gelu_value, preact)
    return pullback(upstream)[0]

def reference(features, tile_values, tile_rows, tile_cols, tile_count, weight, out_grad):
    block_rows = N_COL * SB
    block_cols = N_ROW * SB
    projected = jnp.dot(features, weight, preferred_element_type=jnp.float32).astype(jnp.bfloat16)
    projected_cells = projected.reshape(N_ROW, N_COL, SB, F)

    def forward_row(row_index):

        def grid_cell(col_index, summed):
            source = projected_cells[:, col_index].reshape(block_cols, F)

            def tile_step(slot, running):
                row_tile = tile_rows[row_index, col_index, slot]
                col_tile = tile_cols[row_index, col_index, slot]
                picked = lax.dynamic_slice_in_dim(source, col_tile * TILE, TILE, 0)
                products = jnp.dot(tile_values[row_index, col_index, slot], picked, preferred_element_type=jnp.float32)
                current = lax.dynamic_slice_in_dim(running, row_tile * TILE, TILE, 0)
                return lax.dynamic_update_slice_in_dim(running, current + products, row_tile * TILE, 0)
            running = lax.fori_loop(jnp.int32(0), tile_count[row_index, col_index], tile_step, jnp.zeros((block_rows, F), jnp.float32))
            rounded = lax.optimization_barrier(running.astype(jnp.bfloat16)).astype(jnp.float32)
            return summed + rounded
        return lax.fori_loop(jnp.int32(0), jnp.int32(N_COL), grid_cell, jnp.zeros((block_rows, F), jnp.float32))
    preact = lax.map(forward_row, jnp.arange(N_ROW, dtype=jnp.int32)).reshape(NODES, F)
    activated = gelu_value(preact).astype(jnp.bfloat16)
    cotangent = gelu_backward(preact, out_grad.astype(jnp.float32)).astype(jnp.bfloat16)
    cotangent_rows = cotangent.reshape(N_ROW, block_rows, F)

    def backward_col(col_index):

        def grid_cell(row_index, summed):
            source = cotangent_rows[row_index]

            def tile_step(slot, running):
                row_tile = tile_rows[row_index, col_index, slot]
                col_tile = tile_cols[row_index, col_index, slot]
                picked = lax.dynamic_slice_in_dim(source, row_tile * TILE, TILE, 0)
                products = jnp.dot(tile_values[row_index, col_index, slot].T, picked, preferred_element_type=jnp.float32)
                current = lax.dynamic_slice_in_dim(running, col_tile * TILE, TILE, 0)
                return lax.dynamic_update_slice_in_dim(running, current + products, col_tile * TILE, 0)
            running = lax.fori_loop(jnp.int32(0), tile_count[row_index, col_index], tile_step, jnp.zeros((block_cols, F), jnp.float32))
            rounded = lax.optimization_barrier(running.astype(jnp.bfloat16)).astype(jnp.float32)
            return summed + rounded
        return lax.fori_loop(jnp.int32(0), jnp.int32(N_ROW), grid_cell, jnp.zeros((block_cols, F), jnp.float32))
    pulled_cols = lax.map(backward_col, jnp.arange(N_COL, dtype=jnp.int32))
    pulled = pulled_cols.reshape(N_COL, N_ROW, SB, F).transpose(1, 0, 2, 3).reshape(NODES, F).astype(jnp.bfloat16)
    weight_grad = jnp.dot(features.T, pulled, preferred_element_type=jnp.float32) * NODES ** (-0.5)
    feature_grad = jnp.dot(pulled, weight.T, preferred_element_type=jnp.float32).astype(jnp.bfloat16)
    return (activated, feature_grad, weight_grad)
```

```python
import functools

import jax
import jax.numpy as jnp
from jax import lax
from jax.experimental import pallas as pl
from jax.experimental.pallas import tpu as pltpu
from jax.sharding import Mesh, PartitionSpec as P

F32 = jnp.float32
BF16 = jnp.bfloat16
AXES = ("zl", "y", "c", "x", "zh")
SIZES = (4, 4, 2, 4, 4)
T = 128
F = 256
UNROLL = 4

VMEM = pl.BlockSpec(memory_space=pltpu.VMEM)
SMEM = pl.BlockSpec(memory_space=pltpu.SMEM)


def call(kernel, out_shapes, in_specs, args, flops, scratch=()):
    nbytes = sum(a.size * a.dtype.itemsize for a in args)
    nbytes += sum(s.size * s.dtype.itemsize for s in out_shapes)
    return pl.pallas_call(
        kernel,
        out_shape=out_shapes,
        in_specs=in_specs,
        out_specs=tuple(VMEM for _ in out_shapes),
        scratch_shapes=list(scratch),
        compiler_params=pltpu.CompilerParams(vmem_limit_bytes=24 * 2**20),
        cost_estimate=pl.CostEstimate(flops=flops, bytes_accessed=nbytes, transcendentals=0),
    )(*args)


def sds(*shape, dtype=BF16):
    return jax.ShapeDtypeStruct(shape, dtype)


def dot(a, b, da, db):
    return lax.dot_general(a, b, (((da,), (db,)), ((), ())), preferred_element_type=F32)


def total(ref, *index):
    terms = [ref[(k,) + index].astype(F32) for k in range(ref.shape[0])]
    while len(terms) > 1:
        terms = [a + b for a, b in zip(terms[::2], terms[1::2])]
    return terms[0]


def split(v):
    hi = v.astype(BF16)
    return hi, (v - hi.astype(F32)).astype(BF16)


def over_slots(count, step):
    def group(g, carry):
        for k in range(UNROLL):
            s = g * UNROLL + k
            step(s, s < count)
        return carry

    lax.fori_loop(0, (count + UNROLL - 1) // UNROLL, group, 0)


def forward_kernel(rows, cols, count, me, tiles, own, other, out, acc):
    acc[...] = jnp.zeros_like(acc)
    mine = me[0]

    def step(s, live):
        r, a = rows[s], cols[s]
        k = (a // 2) % 4 * 4 + a // 8
        source = jnp.where(a % 2 == mine, own[k], other[k])
        tile = jnp.where(live, tiles[s], jnp.zeros((), BF16))
        acc[r] += dot(tile, source, 1, 0)

    over_slots(count[0], step)
    out[...] = acc[...].astype(BF16)


def sum_kernel(parts, out):
    out[...] = total(parts).astype(BF16)


def gelu_kernel(parts, weight, upstream, activated, cot, wterm):
    z = total(parts).astype(BF16)
    v = dot(z, weight[...], 1, 0)
    k = 0.7978845608028654
    v2 = v * v
    t = jnp.tanh(k * (v + 0.044715 * (v2 * v)))
    cdf = 0.5 * (1.0 + t)
    activated[...] = (v * cdf).astype(BF16)
    slope = cdf + 0.5 * v * (1.0 - t * t) * (k * (1.0 + 3 * 0.044715 * v2))
    d = (upstream[...].astype(F32) * slope).astype(BF16)
    cot[...] = d
    wterm[...] = dot(z, d, 0, 0).astype(BF16)


def pack_zh_kernel(wparts, cot, out):
    hi, lo = split(total(wparts))
    tail = jnp.concatenate([hi, lo], axis=0)
    for d in range(4):
        out[d, :T] = cot[...]
        out[d, T:] = tail


def pack_x_kernel(parts, out):
    w = total(parts, slice(T, T + 16))
    hi, lo = split(w[:8] + w[8:])
    tail = jnp.concatenate([hi, lo], axis=0)
    for d in range(4):
        for z in range(4):
            out[d, z * T : (z + 1) * T] = parts[z, :T]
        out[d, 4 * T :] = tail


def backward_kernel(rows, cols, count, me, tiles, cots, own, send, acc):
    acc[...] = jnp.zeros_like(acc)
    mine = me[0]

    def step(s, live):
        r, a = rows[s], cols[s]
        k = a % 2 * 16 + (a // 2) % 4 * 4 + a // 8
        source = cots[r // 4, pl.ds(pl.multiple_of(r % 4 * T, T), T)]
        tile = jnp.where(live, tiles[s], jnp.zeros((), BF16))
        acc[k] += dot(tile, source, 0, 0)

    over_slots(count[0], step)
    keep = mine * 16
    give = 16 - keep
    for k in range(16):
        own[k * T : (k + 1) * T] = acc[keep + k].astype(BF16)
        send[k * T : (k + 1) * T] = acc[give + k].astype(BF16)
    w = total(cots, slice(4 * T, 4 * T + 16))
    w = (w[:8] + w[8:]).astype(BF16)
    w = jnp.concatenate([w, w], axis=0)
    own[16 * T :] = w
    send[16 * T :] = w


def pack_y_kernel(me, own, got, out):
    for y in range(4):
        block = slice(y * 4 * T, (y + 1) * 4 * T)
        out[y, : 4 * T] = (own[block].astype(F32) + got[block].astype(F32)).astype(BF16)
    a = own[16 * T :].astype(F32)
    b = got[16 * T :].astype(F32)
    row = lax.broadcasted_iota(jnp.int32, (16, F), 0)
    tail = jnp.where(row // 8 == me[0], a, b).astype(BF16)
    for y in range(4):
        out[y, 4 * T :] = tail


def pack_zl_kernel(parts, out):
    for d in range(4):
        out[d, :T] = total(parts, slice(d * T, (d + 1) * T)).astype(BF16)
        for y in range(4):
            out[d, T + 16 * y : T + 16 * (y + 1)] = parts[y, 4 * T :]


def last_kernel(scale, parts, weight, feature_grad, weight_grad):
    pulled = total(parts, slice(0, T)).astype(BF16)
    feature_grad[...] = dot(pulled, weight[...], 1, 1).astype(BF16)
    for z in range(4):
        weight_grad[z * 64 : (z + 1) * 64] = parts[z, T:].astype(F32) * scale


def exchange(v, axis):
    return lax.all_to_all(v, axis, 0, 0)


def swap(v):
    return lax.ppermute(v, "c", [(0, 1), (1, 0)])


def body(features, tile_values, tile_rows, tile_cols, tile_count, weight, out_grad):
    tiles = tile_values[0, 0]
    rows, cols, count = tile_rows[0, 0], tile_cols[0, 0], tile_count[0]
    me = lax.axis_index("c").astype(jnp.int32).reshape(1)
    slots = tiles.shape[0]
    tile_flops = slots * 2 * T * T * F

    got = exchange(jnp.broadcast_to(features, (4, T, F)), "zl").reshape(4 * T, F)
    got = exchange(jnp.broadcast_to(got, (4, 4 * T, F)), "y").reshape(16, T, F)
    other = swap(got)

    (partial,) = call(
        forward_kernel,
        (sds(16, T, F),),
        [SMEM] * 4 + [VMEM] * 3,
        (rows, cols, count, me, tiles, got, other),
        tile_flops,
        [pltpu.VMEM((16, T, F), F32)],
    )
    parts = exchange(partial.reshape(4, 4 * T, F), "x")
    (summed,) = call(sum_kernel, (sds(4 * T, F),), [VMEM], (parts,), 2**20)
    parts = exchange(summed.reshape(4, T, F), "zh")
    activated, cot, wterm = call(
        gelu_kernel,
        (sds(T, F), sds(T, F), sds(F, F)),
        [VMEM] * 3,
        (parts, weight, out_grad),
        8 * T * F * F,
    )
    wparts = exchange(wterm.reshape(32, 8, F), ("zl", "y", "c"))

    (packed,) = call(pack_zh_kernel, (sds(4, T + 16, F),), [VMEM] * 2, (wparts, cot), 2**20)
    parts = exchange(packed, "zh")
    (packed,) = call(pack_x_kernel, (sds(4, 4 * T + 16, F),), [VMEM], (parts,), 2**20)
    cots = exchange(packed, "x")

    own, send = call(
        backward_kernel,
        (sds(16 * T + 16, F), sds(16 * T + 16, F)),
        [SMEM] * 4 + [VMEM] * 2,
        (rows, cols, count, me, tiles, cots),
        tile_flops,
        [pltpu.VMEM((32, T, F), F32)],
    )
    recv = swap(send)
    (packed,) = call(
        pack_y_kernel, (sds(4, 4 * T + 16, F),), [SMEM] + [VMEM] * 2, (me, own, recv), 2**20
    )
    parts = exchange(packed, "y")
    (packed,) = call(pack_zl_kernel, (sds(4, T + 64, F),), [VMEM], (parts,), 2**20)
    parts = exchange(packed, "zl")
    scale = float(T * 512) ** -0.5
    feature_grad, weight_grad = call(
        functools.partial(last_kernel, scale),
        (sds(T, F), sds(F, F, dtype=F32)),
        [VMEM] * 2,
        (parts, weight),
        2 * T * F * F,
    )
    return activated, feature_grad, weight_grad


def solution(mesh):
    fine = Mesh(mesh.devices.reshape(SIZES), AXES)
    row, col = AXES[:3], AXES[3:]
    placed = (
        P(AXES, None),
        P(row, col, None, None, None),
        P(row, col, None),
        P(row, col, None),
        P(row, col),
        P(),
        P(AXES, None),
    )
    return jax.shard_map(
        body,
        mesh=fine,
        in_specs=placed,
        out_specs=(P(AXES, None), P(AXES, None), P()),
        check_vma=False,
    )
```

```python
import functools

import jax
import jax.numpy as jnp
from jax import lax
from jax.experimental import pallas as pl
from jax.experimental.pallas import tpu as pltpu
from jax.sharding import Mesh, PartitionSpec as P

F32 = jnp.float32
BF16 = jnp.bfloat16
AXES = ("zl", "y", "c", "x", "zh")
SIZES = (4, 4, 2, 4, 4)
T = 128
F = 256
UNROLL = 4

VMEM = pl.BlockSpec(memory_space=pltpu.VMEM)
SMEM = pl.BlockSpec(memory_space=pltpu.SMEM)


def call(kernel, out_shapes, in_specs, args, flops, scratch=()):
    nbytes = sum(a.size * a.dtype.itemsize for a in args)
    nbytes += sum(s.size * s.dtype.itemsize for s in out_shapes)
    return pl.pallas_call(
        kernel,
        out_shape=out_shapes,
        in_specs=in_specs,
        out_specs=tuple(VMEM for _ in out_shapes),
        scratch_shapes=list(scratch),
        compiler_params=pltpu.CompilerParams(vmem_limit_bytes=24 * 2**20),
        cost_estimate=pl.CostEstimate(flops=flops, bytes_accessed=nbytes, transcendentals=0),
    )(*args)


def sds(*shape, dtype=BF16):
    return jax.ShapeDtypeStruct(shape, dtype)


def dot(a, b, da, db):
    return lax.dot_general(a, b, (((da,), (db,)), ((), ())), preferred_element_type=F32)


def total(ref, *index):
    terms = [ref[(k,) + index].astype(F32) for k in range(ref.shape[0])]
    while len(terms) > 1:
        terms = [a + b for a, b in zip(terms[::2], terms[1::2])]
    return terms[0]


def over_slots(count, step):
    def group(g, carry):
        for k in range(UNROLL):
            s = g * UNROLL + k
            step(s, s < count)
        return carry

    lax.fori_loop(0, (count + UNROLL - 1) // UNROLL, group, 0)


def forward_kernel(rows, cols, count, me, tiles, own, other, out, acc):
    acc[...] = jnp.zeros_like(acc)
    mine = me[0]

    def step(s, live):
        r, a = rows[s], cols[s]
        k = (a // 2) % 4 * 4 + a // 8
        source = jnp.where(a % 2 == mine, own[k], other[k])
        tile = jnp.where(live, tiles[s], jnp.zeros((), BF16))
        acc[r] += dot(tile, source, 1, 0)

    over_slots(count[0], step)
    out[...] = acc[...].astype(BF16)


def sum_kernel(parts, out):
    out[...] = total(parts).astype(BF16)


def gelu_kernel(parts, weight, upstream, activated, cot, wterm):
    z = total(parts).astype(BF16)
    v = dot(z, weight[...], 1, 0)
    k = 0.7978845608028654
    v2 = v * v
    t = jnp.tanh(k * (v + 0.044715 * (v2 * v)))
    cdf = 0.5 * (1.0 + t)
    activated[...] = (v * cdf).astype(BF16)
    slope = cdf + 0.5 * v * (1.0 - t * t) * (k * (1.0 + 3 * 0.044715 * v2))
    d = (upstream[...].astype(F32) * slope).astype(BF16)
    cot[...] = d
    wterm[...] = dot(z, d, 0, 0).astype(BF16)


def pack_zh_kernel(wparts, cot, out):
    tail = total(wparts).astype(BF16)
    for d in range(4):
        out[d, :T] = cot[...]
        out[d, T:] = tail


def pack_x_kernel(parts, out):
    tail = total(parts, slice(T, T + 16)).astype(BF16)
    for d in range(4):
        for z in range(4):
            out[d, z * T : (z + 1) * T] = parts[z, :T]
        out[d, 4 * T :] = tail


def backward_kernel(rows, cols, count, me, tiles, cots, own, send, acc):
    acc[...] = jnp.zeros_like(acc)
    mine = me[0]

    def step(s, live):
        r, a = rows[s], cols[s]
        k = a % 2 * 16 + (a // 2) % 4 * 4 + a // 8
        source = cots[r // 4, pl.ds(pl.multiple_of(r % 4 * T, T), T)]
        tile = jnp.where(live, tiles[s], jnp.zeros((), BF16))
        acc[k] += dot(tile, source, 0, 0)

    over_slots(count[0], step)
    keep = mine * 16
    give = 16 - keep
    for k in range(16):
        own[k * T : (k + 1) * T] = acc[keep + k].astype(BF16)
        send[k * T : (k + 1) * T] = acc[give + k].astype(BF16)
    w = total(cots, slice(4 * T, 4 * T + 16)).astype(BF16)
    own[16 * T :] = w
    send[16 * T :] = w


def pack_y_kernel(own, got, out):
    for y in range(4):
        block = slice(y * 4 * T, (y + 1) * 4 * T)
        out[y, : 4 * T] = (own[block].astype(F32) + got[block].astype(F32)).astype(BF16)
    tail = (own[16 * T :].astype(F32) + got[16 * T :].astype(F32)).astype(BF16)
    for y in range(4):
        out[y, 4 * T :] = tail


def pack_zl_kernel(parts, out):
    for d in range(4):
        out[d, :T] = total(parts, slice(d * T, (d + 1) * T)).astype(BF16)
        for y in range(4):
            out[d, T + 16 * y : T + 16 * (y + 1)] = parts[y, 4 * T :]


def last_kernel(scale, parts, weight, feature_grad, weight_grad):
    pulled = total(parts, slice(0, T)).astype(BF16)
    feature_grad[...] = dot(pulled, weight[...], 1, 1).astype(BF16)
    for z in range(4):
        weight_grad[z * 64 : (z + 1) * 64] = parts[z, T:].astype(F32) * scale


def exchange(v, axis):
    return lax.all_to_all(v, axis, 0, 0)


def swap(v):
    return lax.ppermute(v, "c", [(0, 1), (1, 0)])


def body(features, tile_values, tile_rows, tile_cols, tile_count, weight, out_grad):
    tiles = tile_values[0, 0]
    rows, cols, count = tile_rows[0, 0], tile_cols[0, 0], tile_count[0]
    me = lax.axis_index("c").astype(jnp.int32).reshape(1)
    slots = tiles.shape[0]
    tile_flops = slots * 2 * T * T * F

    got = exchange(jnp.broadcast_to(features, (4, T, F)), "zl").reshape(4 * T, F)
    got = exchange(jnp.broadcast_to(got, (4, 4 * T, F)), "y").reshape(16, T, F)
    other = swap(got)

    (partial,) = call(
        forward_kernel,
        (sds(16, T, F),),
        [SMEM] * 4 + [VMEM] * 3,
        (rows, cols, count, me, tiles, got, other),
        tile_flops,
        [pltpu.VMEM((16, T, F), F32)],
    )
    parts = exchange(partial.reshape(4, 4 * T, F), "x")
    (summed,) = call(sum_kernel, (sds(4 * T, F),), [VMEM], (parts,), 2**20)
    parts = exchange(summed.reshape(4, T, F), "zh")
    activated, cot, wterm = call(
        gelu_kernel,
        (sds(T, F), sds(T, F), sds(F, F)),
        [VMEM] * 3,
        (parts, weight, out_grad),
        8 * T * F * F,
    )
    wparts = exchange(wterm.reshape(16, 16, F), ("zl", "y"))

    (packed,) = call(pack_zh_kernel, (sds(4, T + 16, F),), [VMEM] * 2, (wparts, cot), 2**20)
    parts = exchange(packed, "zh")
    (packed,) = call(pack_x_kernel, (sds(4, 4 * T + 16, F),), [VMEM], (parts,), 2**20)
    cots = exchange(packed, "x")

    own, send = call(
        backward_kernel,
        (sds(16 * T + 16, F), sds(16 * T + 16, F)),
        [SMEM] * 4 + [VMEM] * 2,
        (rows, cols, count, me, tiles, cots),
        tile_flops,
        [pltpu.VMEM((32, T, F), F32)],
    )
    recv = swap(send)
    (packed,) = call(
        pack_y_kernel, (sds(4, 4 * T + 16, F),), [VMEM] * 2, (own, recv), 2**20
    )
    parts = exchange(packed, "y")
    (packed,) = call(pack_zl_kernel, (sds(4, T + 64, F),), [VMEM], (parts,), 2**20)
    parts = exchange(packed, "zl")
    scale = float(T * 512) ** -0.5
    feature_grad, weight_grad = call(
        functools.partial(last_kernel, scale),
        (sds(T, F), sds(F, F, dtype=F32)),
        [VMEM] * 2,
        (parts, weight),
        2 * T * F * F,
    )
    return activated, feature_grad, weight_grad


def solution(mesh):
    fine = Mesh(mesh.devices.reshape(SIZES), AXES)
    row, col = AXES[:3], AXES[3:]
    placed = (
        P(AXES, None),
        P(row, col, None, None, None),
        P(row, col, None),
        P(row, col, None),
        P(row, col),
        P(),
        P(AXES, None),
    )
    return jax.shard_map(
        body,
        mesh=fine,
        in_specs=placed,
        out_specs=(P(AXES, None), P(AXES, None), P()),
        check_vma=False,
    )
```

```python
import functools

import jax
import jax.numpy as jnp
from jax import lax
from jax.experimental import pallas as pl
from jax.experimental.pallas import tpu as pltpu
from jax.sharding import Mesh, PartitionSpec as P

F32 = jnp.float32
BF16 = jnp.bfloat16
AXES = ("zl", "y", "c", "x", "zh")
SIZES = (4, 4, 2, 4, 4)
T = 128
F = 256
UNROLL = 4
LAG_F = 3000
LAG_B = 3000
WHO = 0

VMEM = pl.BlockSpec(memory_space=pltpu.VMEM)
SMEM = pl.BlockSpec(memory_space=pltpu.SMEM)


def call(kernel, out_shapes, in_specs, args, flops, scratch=()):
    nbytes = sum(a.size * a.dtype.itemsize for a in args)
    nbytes += sum(s.size * s.dtype.itemsize for s in out_shapes)
    return pl.pallas_call(
        kernel,
        out_shape=out_shapes,
        in_specs=in_specs,
        out_specs=tuple(VMEM for _ in out_shapes),
        scratch_shapes=list(scratch),
        compiler_params=pltpu.CompilerParams(vmem_limit_bytes=24 * 2**20),
        cost_estimate=pl.CostEstimate(flops=flops, bytes_accessed=nbytes, transcendentals=0),
    )(*args)


def sds(*shape, dtype=BF16):
    return jax.ShapeDtypeStruct(shape, dtype)


def dot(a, b, da, db):
    return lax.dot_general(a, b, (((da,), (db,)), ((), ())), preferred_element_type=F32)


def total(ref, *index):
    terms = [ref[(k,) + index].astype(F32) for k in range(ref.shape[0])]
    while len(terms) > 1:
        terms = [a + b for a, b in zip(terms[::2], terms[1::2])]
    return terms[0]


def over_slots(count, step):
    def group(g, carry):
        for k in range(UNROLL):
            s = g * UNROLL + k
            step(s, s < count)
        return carry

    lax.fori_loop(0, (count + UNROLL - 1) // UNROLL, group, 0)


def forward_kernel(rows, cols, count, me, tiles, own, other, out, acc):
    acc[...] = jnp.zeros_like(acc)
    mine = me[0]

    if LAG_F:

        @pl.when(mine == WHO)
        def _():
            pl.delay(LAG_F)

    def step(s, live):
        r, a = rows[s], cols[s]
        k = (a // 2) % 4 * 4 + a // 8
        source = jnp.where(a % 2 == mine, own[k], other[k])
        tile = jnp.where(live, tiles[s], jnp.zeros((), BF16))
        acc[r] += dot(tile, source, 1, 0)

    over_slots(count[0], step)
    out[...] = acc[...].astype(BF16)


def sum_kernel(parts, out):
    out[...] = total(parts).astype(BF16)


def gelu_kernel(parts, weight, upstream, activated, cot, wterm):
    z = total(parts).astype(BF16)
    v = dot(z, weight[...], 1, 0)
    k = 0.7978845608028654
    v2 = v * v
    t = jnp.tanh(k * (v + 0.044715 * (v2 * v)))
    cdf = 0.5 * (1.0 + t)
    activated[...] = (v * cdf).astype(BF16)
    slope = cdf + 0.5 * v * (1.0 - t * t) * (k * (1.0 + 3 * 0.044715 * v2))
    d = (upstream[...].astype(F32) * slope).astype(BF16)
    cot[...] = d
    wterm[...] = dot(z, d, 0, 0).astype(BF16)


def pack_zh_kernel(wparts, cot, out):
    tail = total(wparts).astype(BF16)
    for d in range(4):
        out[d, :T] = cot[...]
        out[d, T:] = tail


def pack_x_kernel(parts, out):
    tail = total(parts, slice(T, T + 16)).astype(BF16)
    for d in range(4):
        for z in range(4):
            out[d, z * T : (z + 1) * T] = parts[z, :T]
        out[d, 4 * T :] = tail


def backward_kernel(rows, cols, count, me, tiles, cots, own, send, acc):
    acc[...] = jnp.zeros_like(acc)
    mine = me[0]

    def step(s, live):
        r, a = rows[s], cols[s]
        k = a % 2 * 16 + (a // 2) % 4 * 4 + a // 8
        source = cots[r // 4, pl.ds(pl.multiple_of(r % 4 * T, T), T)]
        tile = jnp.where(live, tiles[s], jnp.zeros((), BF16))
        acc[k] += dot(tile, source, 0, 0)

    over_slots(count[0], step)
    keep = mine * 16
    give = 16 - keep
    for k in range(16):
        own[k * T : (k + 1) * T] = acc[keep + k].astype(BF16)
        send[k * T : (k + 1) * T] = acc[give + k].astype(BF16)
    w = total(cots, slice(4 * T, 4 * T + 16)).astype(BF16)
    own[16 * T :] = w
    send[16 * T :] = w


def pack_y_kernel(me, own, got, out):
    if LAG_B:

        @pl.when(me[0] == WHO)
        def _():
            pl.delay(LAG_B)

    for y in range(4):
        block = slice(y * 4 * T, (y + 1) * 4 * T)
        out[y, : 4 * T] = (own[block].astype(F32) + got[block].astype(F32)).astype(BF16)
    tail = (own[16 * T :].astype(F32) + got[16 * T :].astype(F32)).astype(BF16)
    for y in range(4):
        out[y, 4 * T :] = tail


def pack_zl_kernel(parts, out):
    for d in range(4):
        out[d, :T] = total(parts, slice(d * T, (d + 1) * T)).astype(BF16)
        for y in range(4):
            out[d, T + 16 * y : T + 16 * (y + 1)] = parts[y, 4 * T :]


def last_kernel(scale, parts, weight, feature_grad, weight_grad):
    pulled = total(parts, slice(0, T)).astype(BF16)
    feature_grad[...] = dot(pulled, weight[...], 1, 1).astype(BF16)
    for z in range(4):
        weight_grad[z * 64 : (z + 1) * 64] = parts[z, T:].astype(F32) * scale


def exchange(v, axis):
    return lax.all_to_all(v, axis, 0, 0)


def swap(v):
    return lax.ppermute(v, "c", [(0, 1), (1, 0)])


def body(features, tile_values, tile_rows, tile_cols, tile_count, weight, out_grad):
    tiles = tile_values[0, 0]
    rows, cols, count = tile_rows[0, 0], tile_cols[0, 0], tile_count[0]
    me = lax.axis_index("c").astype(jnp.int32).reshape(1)
    slots = tiles.shape[0]
    tile_flops = slots * 2 * T * T * F

    got = exchange(jnp.broadcast_to(features, (4, T, F)), "zl").reshape(4 * T, F)
    got = exchange(jnp.broadcast_to(got, (4, 4 * T, F)), "y").reshape(16, T, F)
    other = swap(got)

    (partial,) = call(
        forward_kernel,
        (sds(16, T, F),),
        [SMEM] * 4 + [VMEM] * 3,
        (rows, cols, count, me, tiles, got, other),
        tile_flops,
        [pltpu.VMEM((16, T, F), F32)],
    )
    parts = exchange(partial.reshape(4, 4 * T, F), "x")
    (summed,) = call(sum_kernel, (sds(4 * T, F),), [VMEM], (parts,), 2**20)
    parts = exchange(summed.reshape(4, T, F), "zh")
    activated, cot, wterm = call(
        gelu_kernel,
        (sds(T, F), sds(T, F), sds(F, F)),
        [VMEM] * 3,
        (parts, weight, out_grad),
        8 * T * F * F,
    )
    wparts = exchange(wterm.reshape(16, 16, F), ("zl", "y"))

    (packed,) = call(pack_zh_kernel, (sds(4, T + 16, F),), [VMEM] * 2, (wparts, cot), 2**20)
    parts = exchange(packed, "zh")
    (packed,) = call(pack_x_kernel, (sds(4, 4 * T + 16, F),), [VMEM], (parts,), 2**20)
    cots = exchange(packed, "x")

    own, send = call(
        backward_kernel,
        (sds(16 * T + 16, F), sds(16 * T + 16, F)),
        [SMEM] * 4 + [VMEM] * 2,
        (rows, cols, count, me, tiles, cots),
        tile_flops,
        [pltpu.VMEM((32, T, F), F32)],
    )
    recv = swap(send)
    (packed,) = call(
        pack_y_kernel, (sds(4, 4 * T + 16, F),), [SMEM] + [VMEM] * 2, (me, own, recv), 2**20
    )
    parts = exchange(packed, "y")
    (packed,) = call(pack_zl_kernel, (sds(4, T + 64, F),), [VMEM], (parts,), 2**20)
    parts = exchange(packed, "zl")
    scale = float(T * 512) ** -0.5
    feature_grad, weight_grad = call(
        functools.partial(last_kernel, scale),
        (sds(T, F), sds(F, F, dtype=F32)),
        [VMEM] * 2,
        (parts, weight),
        2 * T * F * F,
    )
    return activated, feature_grad, weight_grad


def solution(mesh):
    fine = Mesh(mesh.devices.reshape(SIZES), AXES)
    row, col = AXES[:3], AXES[3:]
    placed = (
        P(AXES, None),
        P(row, col, None, None, None),
        P(row, col, None),
        P(row, col, None),
        P(row, col),
        P(),
        P(AXES, None),
    )
    return jax.shard_map(
        body,
        mesh=fine,
        in_specs=placed,
        out_specs=(P(AXES, None), P(AXES, None), P()),
        check_vma=False,
    )
```

```python
import functools

import jax
import jax.numpy as jnp
from jax import lax
from jax.experimental import pallas as pl
from jax.experimental.pallas import tpu as pltpu
from jax.sharding import Mesh, PartitionSpec as P

F32 = jnp.float32
BF16 = jnp.bfloat16
AXES = ("zl", "y", "c", "x", "zh")
SIZES = (4, 4, 2, 4, 4)
T = 128
F = 256
UNROLL = 4
LAG_F = 3000
LAG_B = 3000

VMEM = pl.BlockSpec(memory_space=pltpu.VMEM)
SMEM = pl.BlockSpec(memory_space=pltpu.SMEM)


def call(kernel, out_shapes, in_specs, args, flops, scratch=(), out_specs=None, aliases={}):
    nbytes = sum(a.size * a.dtype.itemsize for a in args)
    nbytes += sum(s.size * s.dtype.itemsize for s in out_shapes)
    return pl.pallas_call(
        kernel,
        out_shape=out_shapes,
        in_specs=in_specs,
        out_specs=out_specs or tuple(VMEM for _ in out_shapes),
        input_output_aliases=aliases,
        scratch_shapes=list(scratch),
        compiler_params=pltpu.CompilerParams(vmem_limit_bytes=24 * 2**20),
        cost_estimate=pl.CostEstimate(flops=flops, bytes_accessed=nbytes, transcendentals=0),
    )(*args)


def sds(*shape, dtype=BF16):
    return jax.ShapeDtypeStruct(shape, dtype)


def dot(a, b, da, db):
    return lax.dot_general(a, b, (((da,), (db,)), ((), ())), preferred_element_type=F32)


def lag(me, amount):
    @pl.when(me[0] == 0)
    def _():
        pl.delay(amount)


def total(ref, *index):
    terms = [ref[(k,) + index].astype(F32) for k in range(ref.shape[0])]
    while len(terms) > 1:
        terms = [a + b for a, b in zip(terms[::2], terms[1::2])]
    return terms[0]


def half_index(col_tile):
    return (col_tile // 2) % 4 * 4 + col_tile // 8


def over_slots(count, near, order, step):
    def group(g, carry):
        for k in range(UNROLL):
            i = g * UNROLL + k
            step(order[31 - i if near else i], i < count)
        return carry

    lax.fori_loop(0, (count + UNROLL - 1) // UNROLL, group, 0)


def near_kernel(rows, cols, count, me, tiles, own, acc, order, far):
    acc[...] = jnp.zeros_like(acc)
    mine = me[0]
    for i in range(32):
        order[i] = 0

    def place(s, n_far):
        is_far = (cols[s] % 2 != mine).astype(jnp.int32)
        order[jnp.where(is_far == 1, n_far, 31 - (s - n_far))] = s
        return n_far + is_far

    n_far = lax.fori_loop(0, count[0], place, jnp.int32(0))
    far[0] = n_far

    def step(s, live):
        tile = jnp.where(live, tiles[s], jnp.zeros((), BF16))
        acc[rows[s]] += dot(tile, own[half_index(cols[s])], 1, 0)

    over_slots(count[0] - n_far, True, order, step)


def far_kernel(rows, cols, me, order, far, tiles, other, given, out, acc):
    def step(s, live):
        tile = jnp.where(live, tiles[s], jnp.zeros((), BF16))
        acc[rows[s]] += dot(tile, other[half_index(cols[s])], 1, 0)

    over_slots(far[0], False, order, step)
    lag(me, LAG_F)
    out[...] = acc[...].astype(BF16)


def sum_kernel(parts, out):
    out[...] = total(parts).astype(BF16)


def gelu_kernel(parts, weight, upstream, activated, cot, wterm):
    z = total(parts).astype(BF16)
    v = dot(z, weight[...], 1, 0)
    k = 0.7978845608028654
    v2 = v * v
    t = jnp.tanh(k * (v + 0.044715 * (v2 * v)))
    cdf = 0.5 * (1.0 + t)
    activated[...] = (v * cdf).astype(BF16)
    slope = cdf + 0.5 * v * (1.0 - t * t) * (k * (1.0 + 3 * 0.044715 * v2))
    d = (upstream[...].astype(F32) * slope).astype(BF16)
    cot[...] = d
    wterm[...] = dot(z, d, 0, 0).astype(BF16)


def pack_zh_kernel(wparts, cot, out):
    tail = total(wparts).astype(BF16)
    for d in range(4):
        out[d, :T] = cot[...]
        out[d, T:] = tail


def pack_x_kernel(parts, out):
    tail = total(parts, slice(T, T + 16)).astype(BF16)
    for d in range(4):
        for z in range(4):
            out[d, z * T : (z + 1) * T] = parts[z, :T]
        out[d, 4 * T :] = tail


def backward_kernel(near, rows, cols, count, order, far, tiles, cots, out, acc):
    acc[...] = jnp.zeros_like(acc)

    def step(s, live):
        r = rows[s]
        source = cots[r // 4, pl.ds(pl.multiple_of(r % 4 * T, T), T)]
        tile = jnp.where(live, tiles[s], jnp.zeros((), BF16))
        acc[half_index(cols[s])] += dot(tile, source, 0, 0)

    over_slots(count[0] - far[0] if near else far[0], near, order, step)
    for k in range(16):
        out[k * T : (k + 1) * T] = acc[k].astype(BF16)
    out[16 * T :] = total(cots, slice(4 * T, 4 * T + 16)).astype(BF16)


def pack_y_kernel(me, own, got, out):
    lag(me, LAG_B)
    for y in range(4):
        block = slice(y * 4 * T, (y + 1) * 4 * T)
        out[y, : 4 * T] = (own[block].astype(F32) + got[block].astype(F32)).astype(BF16)
    tail = (own[16 * T :].astype(F32) + got[16 * T :].astype(F32)).astype(BF16)
    for y in range(4):
        out[y, 4 * T :] = tail


def pack_zl_kernel(parts, out):
    for d in range(4):
        out[d, :T] = total(parts, slice(d * T, (d + 1) * T)).astype(BF16)
        for y in range(4):
            out[d, T + 16 * y : T + 16 * (y + 1)] = parts[y, 4 * T :]


def last_kernel(scale, parts, weight, feature_grad, weight_grad):
    pulled = total(parts, slice(0, T)).astype(BF16)
    feature_grad[...] = dot(pulled, weight[...], 1, 1).astype(BF16)
    for z in range(4):
        weight_grad[z * 64 : (z + 1) * 64] = parts[z, T:].astype(F32) * scale


def exchange(v, axis):
    return lax.all_to_all(v, axis, 0, 0)


def swap(v):
    return lax.ppermute(v, "c", [(0, 1), (1, 0)])


def body(features, tile_values, tile_rows, tile_cols, tile_count, weight, out_grad):
    tiles = tile_values[0, 0]
    rows, cols, count = tile_rows[0, 0], tile_cols[0, 0], tile_count[0]
    me = lax.axis_index("c").astype(jnp.int32).reshape(1)
    slots = tiles.shape[0]
    tile_flops = slots * 2 * T * T * F

    got = exchange(jnp.broadcast_to(features, (4, T, F)), "zl").reshape(4 * T, F)
    got = exchange(jnp.broadcast_to(got, (4, 4 * T, F)), "y").reshape(16, T, F)
    other = swap(got)
    acc, order, far = call(
        near_kernel,
        (sds(16, T, F, dtype=F32), sds(32, dtype=jnp.int32), sds(1, dtype=jnp.int32)),
        [SMEM] * 4 + [VMEM] * 2,
        (rows, cols, count, me, tiles, got),
        tile_flops,
        out_specs=(VMEM, SMEM, SMEM),
    )
    partial, _ = call(
        far_kernel,
        (sds(16, T, F), sds(16, T, F, dtype=F32)),
        [SMEM] * 5 + [VMEM] * 3,
        (rows, cols, me, order, far, tiles, other, acc),
        tile_flops,
        aliases={7: 1},
    )
    parts = exchange(partial.reshape(4, 4 * T, F), "x")
    (summed,) = call(sum_kernel, (sds(4 * T, F),), [VMEM], (parts,), 2**20)
    parts = exchange(summed.reshape(4, T, F), "zh")
    activated, cot, wterm = call(
        gelu_kernel,
        (sds(T, F), sds(T, F), sds(F, F)),
        [VMEM] * 3,
        (parts, weight, out_grad),
        8 * T * F * F,
    )
    wparts = exchange(wterm.reshape(16, 16, F), ("zl", "y"))

    (packed,) = call(pack_zh_kernel, (sds(4, T + 16, F),), [VMEM] * 2, (wparts, cot), 2**20)
    parts = exchange(packed, "zh")
    (packed,) = call(pack_x_kernel, (sds(4, 4 * T + 16, F),), [VMEM], (parts,), 2**20)
    cots = exchange(packed, "x")

    send, own = (
        call(
            functools.partial(backward_kernel, near),
            (sds(16 * T + 16, F),),
            [SMEM] * 5 + [VMEM] * 2,
            (rows, cols, count, order, far, tiles, cots),
            tile_flops,
            [pltpu.VMEM((16, T, F), F32)],
        )[0]
        for near in (False, True)
    )
    recv = swap(send)
    (packed,) = call(
        pack_y_kernel, (sds(4, 4 * T + 16, F),), [SMEM] + [VMEM] * 2, (me, own, recv), 2**20
    )
    parts = exchange(packed, "y")
    (packed,) = call(pack_zl_kernel, (sds(4, T + 64, F),), [VMEM], (parts,), 2**20)
    parts = exchange(packed, "zl")
    scale = float(T * 512) ** -0.5
    feature_grad, weight_grad = call(
        functools.partial(last_kernel, scale),
        (sds(T, F), sds(F, F, dtype=F32)),
        [VMEM] * 2,
        (parts, weight),
        2 * T * F * F,
    )
    return activated, feature_grad, weight_grad


def solution(mesh):
    fine = Mesh(mesh.devices.reshape(SIZES), AXES)
    row, col = AXES[:3], AXES[3:]
    placed = (
        P(AXES, None),
        P(row, col, None, None, None),
        P(row, col, None),
        P(row, col, None),
        P(row, col),
        P(),
        P(AXES, None),
    )
    return jax.shard_map(
        body,
        mesh=fine,
        in_specs=placed,
        out_specs=(P(AXES, None), P(AXES, None), P()),
        check_vma=False,
    )
```

```python
import functools

import jax
import jax.numpy as jnp
from jax import lax
from jax.experimental import pallas as pl
from jax.experimental.pallas import tpu as pltpu
from jax.sharding import Mesh, PartitionSpec as P

F32 = jnp.float32
BF16 = jnp.bfloat16
AXES = ("zl", "y", "c", "x", "zh")
SIZES = (4, 4, 2, 4, 4)
T = 128
F = 256
UNROLL = 4
LAG_F = 3000
LAG_B = 3000

VMEM = pl.BlockSpec(memory_space=pltpu.VMEM)
SMEM = pl.BlockSpec(memory_space=pltpu.SMEM)


def call(kernel, out_shapes, in_specs, args, flops, scratch=(), out_specs=None, aliases={}):
    nbytes = sum(a.size * a.dtype.itemsize for a in args)
    nbytes += sum(s.size * s.dtype.itemsize for s in out_shapes)
    return pl.pallas_call(
        kernel,
        out_shape=out_shapes,
        in_specs=in_specs,
        out_specs=out_specs or tuple(VMEM for _ in out_shapes),
        input_output_aliases=aliases,
        scratch_shapes=list(scratch),
        compiler_params=pltpu.CompilerParams(vmem_limit_bytes=24 * 2**20),
        cost_estimate=pl.CostEstimate(flops=flops, bytes_accessed=nbytes, transcendentals=0),
    )(*args)


def sds(*shape, dtype=BF16):
    return jax.ShapeDtypeStruct(shape, dtype)


def dot(a, b, da, db):
    return lax.dot_general(a, b, (((da,), (db,)), ((), ())), preferred_element_type=F32)


def lag(me, amount):
    @pl.when(me == 0)
    def _():
        pl.delay(amount)


def total(ref, *index):
    terms = [ref[(k,) + index].astype(F32) for k in range(ref.shape[0])]
    while len(terms) > 1:
        terms = [a + b for a, b in zip(terms[::2], terms[1::2])]
    return terms[0]


def half_index(col_tile):
    return (col_tile // 2) % 4 * 4 + col_tile // 8


def over_slots(near, plan, tiles, step):
    n_far = plan[96]
    count = plan[97] - n_far if near else n_far

    def group(g, carry):
        for k in range(UNROLL):
            i = g * UNROLL + k
            p = 31 - i if near else i
            tile = jnp.where(i < count, tiles[plan[p]], jnp.zeros((), BF16))
            step(tile, plan[32 + p], plan[64 + p])
        return carry

    lax.fori_loop(0, (count + UNROLL - 1) // UNROLL, group, 0)


def near_kernel(rows, cols, count, me, tiles, own, acc, plan):
    mine = me[0]
    for i in range(96):
        plan[i] = 0

    def place(s, n_far):
        far = (cols[s] % 2 != mine).astype(jnp.int32)
        p = jnp.where(far == 1, n_far, 31 - (s - n_far))
        plan[p] = s
        plan[32 + p] = rows[s]
        plan[64 + p] = half_index(cols[s])
        return n_far + far

    plan[96] = lax.fori_loop(0, count[0], place, jnp.int32(0))
    plan[97] = count[0]
    plan[98] = mine
    acc[...] = jnp.zeros_like(acc)

    def step(tile, r, k):
        acc[r] += dot(tile, own[k], 1, 0)

    over_slots(True, plan, tiles, step)


def far_kernel(plan, tiles, other, given, out, acc):
    def step(tile, r, k):
        acc[r] += dot(tile, other[k], 1, 0)

    over_slots(False, plan, tiles, step)
    lag(plan[98], LAG_F)
    out[...] = acc[...].astype(BF16)


def sum_kernel(parts, out):
    out[...] = total(parts).astype(BF16)


def gelu_kernel(parts, weight, upstream, activated, cot, wterm):
    z = total(parts).astype(BF16)
    v = dot(z, weight[...], 1, 0)
    k = 0.7978845608028654
    v2 = v * v
    t = jnp.tanh(k * (v + 0.044715 * (v2 * v)))
    cdf = 0.5 * (1.0 + t)
    activated[...] = (v * cdf).astype(BF16)
    slope = cdf + 0.5 * v * (1.0 - t * t) * (k * (1.0 + 3 * 0.044715 * v2))
    d = (upstream[...].astype(F32) * slope).astype(BF16)
    cot[...] = d
    wterm[...] = dot(z, d, 0, 0).astype(BF16)


def pack_zh_kernel(wparts, cot, out):
    tail = total(wparts).astype(BF16)
    for d in range(4):
        out[d, :T] = cot[...]
        out[d, T:] = tail


def pack_x_kernel(parts, out):
    tail = total(parts, slice(T, T + 16)).astype(BF16)
    for d in range(4):
        for z in range(4):
            out[d, z * T : (z + 1) * T] = parts[z, :T]
        out[d, 4 * T :] = tail


def backward_kernel(near, plan, tiles, cots, out, acc):
    acc[...] = jnp.zeros_like(acc)

    def step(tile, r, k):
        source = cots[r // 4, pl.ds(pl.multiple_of(r % 4 * T, T), T)]
        acc[k] += dot(tile, source, 0, 0)

    over_slots(near, plan, tiles, step)
    for k in range(16):
        out[k * T : (k + 1) * T] = acc[k].astype(BF16)
    out[16 * T :] = total(cots, slice(4 * T, 4 * T + 16)).astype(BF16)


def pack_y_kernel(me, own, got, out):
    lag(me[0], LAG_B)
    for y in range(4):
        block = slice(y * 4 * T, (y + 1) * 4 * T)
        out[y, : 4 * T] = (own[block].astype(F32) + got[block].astype(F32)).astype(BF16)
    tail = (own[16 * T :].astype(F32) + got[16 * T :].astype(F32)).astype(BF16)
    for y in range(4):
        out[y, 4 * T :] = tail


def pack_zl_kernel(parts, out):
    for d in range(4):
        out[d, :T] = total(parts, slice(d * T, (d + 1) * T)).astype(BF16)
        for y in range(4):
            out[d, T + 16 * y : T + 16 * (y + 1)] = parts[y, 4 * T :]


def last_kernel(scale, parts, weight, feature_grad, weight_grad):
    pulled = total(parts, slice(0, T)).astype(BF16)
    feature_grad[...] = dot(pulled, weight[...], 1, 1).astype(BF16)
    for z in range(4):
        weight_grad[z * 64 : (z + 1) * 64] = parts[z, T:].astype(F32) * scale


def exchange(v, axis):
    return lax.all_to_all(v, axis, 0, 0)


def swap(v):
    return lax.ppermute(v, "c", [(0, 1), (1, 0)])


def body(features, tile_values, tile_rows, tile_cols, tile_count, weight, out_grad):
    tiles = tile_values[0, 0]
    rows, cols, count = tile_rows[0, 0], tile_cols[0, 0], tile_count[0]
    me = lax.axis_index("c").astype(jnp.int32).reshape(1)
    slots = tiles.shape[0]
    tile_flops = slots * 2 * T * T * F

    got = exchange(jnp.broadcast_to(features, (4, T, F)), "zl").reshape(4 * T, F)
    got = exchange(jnp.broadcast_to(got, (4, 4 * T, F)), "y").reshape(16, T, F)
    other = swap(got)
    acc, plan = call(
        near_kernel,
        (sds(16, T, F, dtype=F32), sds(128, dtype=jnp.int32)),
        [SMEM] * 4 + [VMEM] * 2,
        (rows, cols, count, me, tiles, got),
        tile_flops,
        out_specs=(VMEM, SMEM),
    )
    partial, _ = call(
        far_kernel,
        (sds(16, T, F), sds(16, T, F, dtype=F32)),
        [SMEM] + [VMEM] * 3,
        (plan, tiles, other, acc),
        tile_flops,
        aliases={3: 1},
    )
    parts = exchange(partial.reshape(4, 4 * T, F), "x")
    (summed,) = call(sum_kernel, (sds(4 * T, F),), [VMEM], (parts,), 2**20)
    parts = exchange(summed.reshape(4, T, F), "zh")
    activated, cot, wterm = call(
        gelu_kernel,
        (sds(T, F), sds(T, F), sds(F, F)),
        [VMEM] * 3,
        (parts, weight, out_grad),
        8 * T * F * F,
    )
    wparts = exchange(wterm.reshape(16, 16, F), ("zl", "y"))

    (packed,) = call(pack_zh_kernel, (sds(4, T + 16, F),), [VMEM] * 2, (wparts, cot), 2**20)
    parts = exchange(packed, "zh")
    (packed,) = call(pack_x_kernel, (sds(4, 4 * T + 16, F),), [VMEM], (parts,), 2**20)
    cots = exchange(packed, "x")

    send, own = (
        call(
            functools.partial(backward_kernel, near),
            (sds(16 * T + 16, F),),
            [SMEM] + [VMEM] * 2,
            (plan, tiles, cots),
            tile_flops,
            [pltpu.VMEM((16, T, F), F32)],
        )[0]
        for near in (False, True)
    )
    recv = swap(send)
    (packed,) = call(
        pack_y_kernel, (sds(4, 4 * T + 16, F),), [SMEM] + [VMEM] * 2, (me, own, recv), 2**20
    )
    parts = exchange(packed, "y")
    (packed,) = call(pack_zl_kernel, (sds(4, T + 64, F),), [VMEM], (parts,), 2**20)
    parts = exchange(packed, "zl")
    scale = float(T * 512) ** -0.5
    feature_grad, weight_grad = call(
        functools.partial(last_kernel, scale),
        (sds(T, F), sds(F, F, dtype=F32)),
        [VMEM] * 2,
        (parts, weight),
        2 * T * F * F,
    )
    return activated, feature_grad, weight_grad


def solution(mesh):
    fine = Mesh(mesh.devices.reshape(SIZES), AXES)
    row, col = AXES[:3], AXES[3:]
    placed = (
        P(AXES, None),
        P(row, col, None, None, None),
        P(row, col, None),
        P(row, col, None),
        P(row, col),
        P(),
        P(AXES, None),
    )
    return jax.shard_map(
        body,
        mesh=fine,
        in_specs=placed,
        out_specs=(P(AXES, None), P(AXES, None), P()),
        check_vma=False,
    )
```

```python
import functools

import jax
import jax.numpy as jnp
from jax import lax
from jax.experimental import pallas as pl
from jax.experimental.pallas import tpu as pltpu
from jax.sharding import Mesh, PartitionSpec as P

F32 = jnp.float32
BF16 = jnp.bfloat16
AXES = ("zl", "y", "c", "x", "zh")
SIZES = (4, 4, 2, 4, 4)
T = 128
F = 256
UNROLL = 8
LAG_F = 3000
LAG_B = 3000
WHO = 0

VMEM = pl.BlockSpec(memory_space=pltpu.VMEM)
SMEM = pl.BlockSpec(memory_space=pltpu.SMEM)


def call(kernel, out_shapes, in_specs, args, flops, scratch=()):
    nbytes = sum(a.size * a.dtype.itemsize for a in args)
    nbytes += sum(s.size * s.dtype.itemsize for s in out_shapes)
    return pl.pallas_call(
        kernel,
        out_shape=out_shapes,
        in_specs=in_specs,
        out_specs=tuple(VMEM for _ in out_shapes),
        scratch_shapes=list(scratch),
        compiler_params=pltpu.CompilerParams(vmem_limit_bytes=24 * 2**20),
        cost_estimate=pl.CostEstimate(flops=flops, bytes_accessed=nbytes, transcendentals=0),
    )(*args)


def sds(*shape, dtype=BF16):
    return jax.ShapeDtypeStruct(shape, dtype)


def dot(a, b, da, db):
    return lax.dot_general(a, b, (((da,), (db,)), ((), ())), preferred_element_type=F32)


def total(ref, *index):
    terms = [ref[(k,) + index].astype(F32) for k in range(ref.shape[0])]
    while len(terms) > 1:
        terms = [a + b for a, b in zip(terms[::2], terms[1::2])]
    return terms[0]


def over_slots(count, step):
    def group(g, carry):
        for k in range(UNROLL):
            s = g * UNROLL + k
            step(s, s < count)
        return carry

    lax.fori_loop(0, (count + UNROLL - 1) // UNROLL, group, 0)


def forward_kernel(rows, cols, count, me, tiles, own, other, out, acc):
    acc[...] = jnp.zeros_like(acc)
    mine = me[0]

    if LAG_F:

        @pl.when(mine == WHO)
        def _():
            pl.delay(LAG_F)

    def step(s, live):
        r, a = rows[s], cols[s]
        k = (a // 2) % 4 * 4 + a // 8
        source = jnp.where(a % 2 == mine, own[k], other[k])
        tile = jnp.where(live, tiles[s], jnp.zeros((), BF16))
        acc[r] += dot(tile, source, 1, 0)

    over_slots(count[0], step)
    out[...] = acc[...].astype(BF16)


def sum_kernel(parts, out):
    out[...] = total(parts).astype(BF16)


def gelu_kernel(parts, weight, upstream, activated, cot, wterm):
    z = total(parts).astype(BF16)
    v = dot(z, weight[...], 1, 0)
    k = 0.7978845608028654
    v2 = v * v
    t = jnp.tanh(k * (v + 0.044715 * (v2 * v)))
    cdf = 0.5 * (1.0 + t)
    activated[...] = (v * cdf).astype(BF16)
    slope = cdf + 0.5 * v * (1.0 - t * t) * (k * (1.0 + 3 * 0.044715 * v2))
    d = (upstream[...].astype(F32) * slope).astype(BF16)
    cot[...] = d
    wterm[...] = dot(z, d, 0, 0).astype(BF16)


def pack_zh_kernel(wparts, cot, out):
    tail = total(wparts).astype(BF16)
    for d in range(4):
        out[d, :T] = cot[...]
        out[d, T:] = tail


def pack_x_kernel(parts, out):
    tail = total(parts, slice(T, T + 16)).astype(BF16)
    for d in range(4):
        for z in range(4):
            out[d, z * T : (z + 1) * T] = parts[z, :T]
        out[d, 4 * T :] = tail


def backward_kernel(rows, cols, count, me, tiles, cots, own, send, acc):
    acc[...] = jnp.zeros_like(acc)
    mine = me[0]

    def step(s, live):
        r, a = rows[s], cols[s]
        k = a % 2 * 16 + (a // 2) % 4 * 4 + a // 8
        source = cots[r // 4, pl.ds(pl.multiple_of(r % 4 * T, T), T)]
        tile = jnp.where(live, tiles[s], jnp.zeros((), BF16))
        acc[k] += dot(tile, source, 0, 0)

    over_slots(count[0], step)
    keep = mine * 16
    give = 16 - keep
    for k in range(16):
        own[k * T : (k + 1) * T] = acc[keep + k].astype(BF16)
        send[k * T : (k + 1) * T] = acc[give + k].astype(BF16)
    w = total(cots, slice(4 * T, 4 * T + 16)).astype(BF16)
    own[16 * T :] = w
    send[16 * T :] = w


def pack_y_kernel(me, own, got, out):
    if LAG_B:

        @pl.when(me[0] == WHO)
        def _():
            pl.delay(LAG_B)

    for y in range(4):
        block = slice(y * 4 * T, (y + 1) * 4 * T)
        out[y, : 4 * T] = (own[block].astype(F32) + got[block].astype(F32)).astype(BF16)
    tail = (own[16 * T :].astype(F32) + got[16 * T :].astype(F32)).astype(BF16)
    for y in range(4):
        out[y, 4 * T :] = tail


def pack_zl_kernel(parts, out):
    for d in range(4):
        out[d, :T] = total(parts, slice(d * T, (d + 1) * T)).astype(BF16)
        for y in range(4):
            out[d, T + 16 * y : T + 16 * (y + 1)] = parts[y, 4 * T :]


def last_kernel(scale, parts, weight, feature_grad, weight_grad):
    pulled = total(parts, slice(0, T)).astype(BF16)
    feature_grad[...] = dot(pulled, weight[...], 1, 1).astype(BF16)
    for z in range(4):
        weight_grad[z * 64 : (z + 1) * 64] = parts[z, T:].astype(F32) * scale


def exchange(v, axis):
    return lax.all_to_all(v, axis, 0, 0)


def swap(v):
    return lax.ppermute(v, "c", [(0, 1), (1, 0)])


def body(features, tile_values, tile_rows, tile_cols, tile_count, weight, out_grad):
    tiles = tile_values[0, 0]
    rows, cols, count = tile_rows[0, 0], tile_cols[0, 0], tile_count[0]
    me = lax.axis_index("c").astype(jnp.int32).reshape(1)
    slots = tiles.shape[0]
    tile_flops = slots * 2 * T * T * F

    got = exchange(jnp.broadcast_to(features, (4, T, F)), "zl").reshape(4 * T, F)
    got = exchange(jnp.broadcast_to(got, (4, 4 * T, F)), "y").reshape(16, T, F)
    other = swap(got)

    (partial,) = call(
        forward_kernel,
        (sds(16, T, F),),
        [SMEM] * 4 + [VMEM] * 3,
        (rows, cols, count, me, tiles, got, other),
        tile_flops,
        [pltpu.VMEM((16, T, F), F32)],
    )
    parts = exchange(partial.reshape(4, 4 * T, F), "x")
    (summed,) = call(sum_kernel, (sds(4 * T, F),), [VMEM], (parts,), 2**20)
    parts = exchange(summed.reshape(4, T, F), "zh")
    activated, cot, wterm = call(
        gelu_kernel,
        (sds(T, F), sds(T, F), sds(F, F)),
        [VMEM] * 3,
        (parts, weight, out_grad),
        8 * T * F * F,
    )
    wparts = exchange(wterm.reshape(16, 16, F), ("zl", "y"))

    (packed,) = call(pack_zh_kernel, (sds(4, T + 16, F),), [VMEM] * 2, (wparts, cot), 2**20)
    parts = exchange(packed, "zh")
    (packed,) = call(pack_x_kernel, (sds(4, 4 * T + 16, F),), [VMEM], (parts,), 2**20)
    cots = exchange(packed, "x")

    own, send = call(
        backward_kernel,
        (sds(16 * T + 16, F), sds(16 * T + 16, F)),
        [SMEM] * 4 + [VMEM] * 2,
        (rows, cols, count, me, tiles, cots),
        tile_flops,
        [pltpu.VMEM((32, T, F), F32)],
    )
    recv = swap(send)
    (packed,) = call(
        pack_y_kernel, (sds(4, 4 * T + 16, F),), [SMEM] + [VMEM] * 2, (me, own, recv), 2**20
    )
    parts = exchange(packed, "y")
    (packed,) = call(pack_zl_kernel, (sds(4, T + 64, F),), [VMEM], (parts,), 2**20)
    parts = exchange(packed, "zl")
    scale = float(T * 512) ** -0.5
    feature_grad, weight_grad = call(
        functools.partial(last_kernel, scale),
        (sds(T, F), sds(F, F, dtype=F32)),
        [VMEM] * 2,
        (parts, weight),
        2 * T * F * F,
    )
    return activated, feature_grad, weight_grad


def solution(mesh):
    fine = Mesh(mesh.devices.reshape(SIZES), AXES)
    row, col = AXES[:3], AXES[3:]
    placed = (
        P(AXES, None),
        P(row, col, None, None, None),
        P(row, col, None),
        P(row, col, None),
        P(row, col),
        P(),
        P(AXES, None),
    )
    return jax.shard_map(
        body,
        mesh=fine,
        in_specs=placed,
        out_specs=(P(AXES, None), P(AXES, None), P()),
        check_vma=False,
    )
```
